32 devices in a mesh: dp: 8 (over z, y), tensor: 4 (over x, core).
Axes of the slice: x: 2, y: 2, z: 4, core: 2. Of those that a mesh axis runs over, the one named last changes fastest.
Arguments:
- tokens: bfloat16 [256, 8192], P('dp'), may hold values from -6 to 6
- output_gradient: bfloat16 [256, 8192], P('dp'), may hold values from -6 to 6
- gate_up_weight: bfloat16 [8192, 2, 26624], P('dp', None, 'tensor'), may hold values from -0.0625 to 0.0625
- down_weight: bfloat16 [26624, 8192], P('tensor', 'dp'), may hold values from -0.0390625 to 0.0390625
- adapter_input_factor: bfloat16 [512, 16, 8192], P('tensor', None, 'dp'), may hold values from -0.0625 to 0.0625
- adapter_output_factor: bfloat16 [512, 16, 26624], P('dp', None, 'tensor'), may hold values from -1.5 to 1.5
- request_token_rows: int32 [8, 4], replicated, may hold values from 1 to 16, 32 in all within a row
- request_adapter: int32 [8, 4], replicated, may hold values from 0 to 511
- adapter_table_row: int32 [512], replicated, may hold values from 0 to 511, each once
Outputs:
- layer_output: bfloat16 [256, 8192], P('tensor', 'dp')
- input_gradient: bfloat16 [256, 8192], P('tensor', 'dp')
- adapter_input_gradient: bfloat16 [512, 16, 8192], P('tensor', None, 'dp')
- adapter_output_gradient: bfloat16 [512, 16, 26624], P('dp', None, 'tensor')
The draws below stay inside these ranges and needn't reach their ends.
Inputs may be any that keep to these rules, and one draw needn't show every extreme that they name: Each row of request_token_rows sums to 32, and its largest entry is 16. `adapter_table_row`: every table row from 0 to 511 appears once.
All inputs are finite; a program needn't handle non-finite values.
Results may differ from the reference program's by a relative error of at most 0.0059.
Values may be sent and summed in bfloat16 or wider, within the bound.
A program may use at most 192 MiB of HBM per device.

```python
import math
import jax
import jax.numpy as jnp
import numpy as np
from jax import lax

MODEL_WIDTH = 8192
HIDDEN_UNITS = 26624
ADAPTER_COUNT = 512
ADAPTER_RANK = 16
REQ_DEV = 4
TOK_DEV = 32
LEN_MAX = 16
TOKENS = 256
N_DP = 8


def set_ends(drawn, key, least, top_value):
    longest = drawn.shape.index(max(drawn.shape))
    spots = []
    for shift in (0, 1):
        where = [jax.random.randint(jax.random.fold_in(key, axis), (), 0, length) for axis, length in enumerate(drawn.shape)]
        where[longest] = (where[longest] + shift) % drawn.shape[longest]
        spots.append(tuple(where))
    return drawn.at[spots[0]].set(least).at[spots[1]].set(top_value)


def block_levels(own_key, dims, cuts, smallest, top_value):
    def one(dim, shards_of):
        draws = jax.random.uniform(jax.random.fold_in(jax.random.fold_in(own_key, 6), dim), (shards_of,), jnp.float32, smallest / len(cuts), top_value / len(cuts))
        return jnp.repeat(jnp.exp(draws), dims[dim] // shards_of).reshape((-1,) + (1,) * (len(dims) - dim - 1))

    loudness = one(*cuts[0])
    for cut in cuts[1:]:
        loudness = loudness * one(*cut)
    return loudness


def length_profile(count, total, bound, lean):
    portions = [(1 << 20) // math.isqrt(standing ** lean) + 1 for standing in range(2, count + 1)]
    rest, holding = total - bound - (count - 1), [1] * (count - 1)
    while rest > 0:
        movable = [i for i in range(count - 1) if holding[i] < bound]
        whole, left = sum([portions[i] for i in movable]), rest
        for i in movable:
            more = min(bound - holding[i], max(1, left * portions[i] // whole), rest)
            holding[i] = holding[i] + more
            rest = rest - more
    return np.array([bound] + holding)


def uneven(rng, amount, total, limit, slope):
    if amount == 2:
        one = jax.random.randint(rng, (), max(1, total - limit), min(limit, total - 1) + 1)
        return jnp.stack([one, total - one])
    tallies = jnp.asarray(length_profile(amount, total, limit, slope), jnp.int32)
    couples = (amount - 1) // 2
    giver, taker = tallies[1:1 + 2 * couples:2], tallies[2:2 + 2 * couples:2]
    margin = jnp.minimum(giver - 1, limit - taker)
    passed = jax.random.randint(jax.random.fold_in(rng, 1), (couples,), 0, 1 << 20) % (margin + 1)
    tallies = tallies.at[1:1 + 2 * couples:2].set(giver - passed).at[2:2 + 2 * couples:2].set(taker + passed)
    return tallies[jax.random.permutation(jax.random.fold_in(rng, 2), amount)]


def bell_draw(stream_key, dims, width, reach, cuts=(), held_as=jnp.bfloat16):
    level = block_levels(stream_key, dims, cuts, -0.22, 0.18) if cuts else 1.0
    values = jax.random.normal(stream_key, dims, jnp.float32) * width * level
    return jnp.minimum(jnp.maximum(values, -reach), reach).astype(held_as)


def setup_inputs(seed: int = 0) -> dict:
    arg_keys = jax.random.split(jax.random.key(seed), 10)
    tokens = bell_draw(arg_keys[0], (TOKENS, MODEL_WIDTH), 1.0, 6.0, ((0, 8),))
    output_gradient = bell_draw(arg_keys[1], (TOKENS, MODEL_WIDTH), 1.0, 6.0, ((0, 8),))
    gate_up_weight = bell_draw(arg_keys[2], (MODEL_WIDTH, 2, HIDDEN_UNITS), MODEL_WIDTH ** -0.5, 0.0625, ((0, 8), (2, 4)))
    down_weight = bell_draw(arg_keys[3], (HIDDEN_UNITS, MODEL_WIDTH), HIDDEN_UNITS ** -0.5, 0.0390625, ((0, 4), (1, 8)))
    adapter_input_factor = bell_draw(arg_keys[4], (ADAPTER_COUNT, ADAPTER_RANK, MODEL_WIDTH), MODEL_WIDTH ** -0.5, 0.0625, ((0, 4), (2, 8)))
    adapter_output_factor = bell_draw(arg_keys[5], (ADAPTER_COUNT, ADAPTER_RANK, HIDDEN_UNITS), ADAPTER_RANK ** -0.5, 1.5, ((0, 8), (2, 4)))
    request_token_rows = jax.vmap(lambda own: uneven(own, REQ_DEV, TOK_DEV, LEN_MAX, 2))(jax.random.split(arg_keys[6], N_DP)).reshape((N_DP, REQ_DEV)).astype(jnp.int32)
    request_adapter = set_ends(jax.random.randint(arg_keys[7], (N_DP, REQ_DEV), 0, ADAPTER_COUNT), jax.random.fold_in(arg_keys[7], 1), 0, ADAPTER_COUNT - 1).astype(jnp.int32)
    adapter_table_row = jax.random.permutation(arg_keys[8], ADAPTER_COUNT).astype(jnp.int32)
    return dict(tokens=tokens, output_gradient=output_gradient, gate_up_weight=gate_up_weight, down_weight=down_weight, adapter_input_factor=adapter_input_factor, adapter_output_factor=adapter_output_factor, request_token_rows=request_token_rows, request_adapter=request_adapter, adapter_table_row=adapter_table_row)


adapter_scale = 0.5


def row_slots(request_token_rows, request_adapter, adapter_table_row, group_rows):
    request_count = request_token_rows.shape[1]
    run_ends = jnp.cumsum(request_token_rows, axis=1).astype(jnp.int32)
    position = jnp.arange(group_rows, dtype=jnp.int32)
    request_of = jnp.sum((run_ends[:, None, :] <= position[None, :, None]).astype(jnp.int32), axis=2).astype(jnp.int32)
    request_ids = jnp.arange(request_count, dtype=jnp.int32)
    adapter_of = jnp.sum(jnp.where(request_of[:, :, None] == request_ids[None, None, :], request_adapter[:, None, :], 0), axis=2).astype(jnp.int32)
    adapter_ids = jnp.arange(adapter_table_row.shape[0], dtype=jnp.int32)
    flat_adapter = adapter_of.reshape(-1)
    return jnp.sum(jnp.where(flat_adapter[:, None] == adapter_ids[None, :], adapter_table_row[None, :], 0), axis=1).astype(jnp.int32)


def reference(tokens, output_gradient, gate_up_weight, down_weight, adapter_input_factor, adapter_output_factor, request_token_rows, request_adapter, adapter_table_row):
    groups = request_token_rows.shape[0]
    group_rows = tokens.shape[0] // groups
    slot_of = row_slots(request_token_rows, request_adapter, adapter_table_row, group_rows)
    table_row_blocks = slot_of.reshape(groups, group_rows)
    token_blocks = tokens.reshape(groups, group_rows, tokens.shape[1])

    def codes_of(block):
        token_row_block, table_row_list = block
        return jnp.einsum("ulq,uq->ul", adapter_input_factor[table_row_list].astype(jnp.float32), token_row_block.astype(jnp.float32))

    codes_total_sum = lax.map(codes_of, (token_blocks, table_row_blocks)).reshape(tokens.shape[0], ADAPTER_RANK)
    code_low = codes_total_sum.astype(jnp.bfloat16)
    code_blocks = code_low.reshape(groups, group_rows, ADAPTER_RANK)

    def lift_of(block):
        codes_per_row, table_row_list = block
        return jnp.einsum("uz,uzv->uv", codes_per_row.astype(jnp.float32), adapter_output_factor[table_row_list].astype(jnp.float32))

    raised_codes = lax.map(lift_of, (code_blocks, table_row_blocks)).reshape(tokens.shape[0], HIDDEN_UNITS)
    gate_pre = jnp.dot(tokens, gate_up_weight[:, 0, :], preferred_element_type=jnp.float32)
    up_activation = jnp.dot(tokens, gate_up_weight[:, 1, :], preferred_element_type=jnp.float32) + adapter_scale * raised_codes
    sigmoid_gate = jax.nn.sigmoid(gate_pre)
    hidden = (gate_pre * sigmoid_gate * up_activation).astype(jnp.bfloat16)
    layer_output = jnp.dot(hidden, down_weight, preferred_element_type=jnp.float32).astype(jnp.bfloat16)
    hidden_grad = jnp.dot(output_gradient, down_weight.T, preferred_element_type=jnp.float32)
    gate_grad = (hidden_grad * up_activation * sigmoid_gate * (1.0 + gate_pre * (1.0 - sigmoid_gate))).astype(jnp.bfloat16)
    up_grad = (hidden_grad * gate_pre * sigmoid_gate).astype(jnp.bfloat16)
    up_weight_blocks = up_grad.reshape(groups, group_rows, HIDDEN_UNITS)

    def backward_codes(block):
        up_weight_rows, table_row_list = block
        return jnp.einsum("lb,lhb->lh", up_weight_rows.astype(jnp.float32), adapter_output_factor[table_row_list].astype(jnp.float32))

    codes_gradient = adapter_scale * lax.map(backward_codes, (up_weight_blocks, table_row_blocks)).reshape(tokens.shape[0], ADAPTER_RANK)
    code_grad_low = codes_gradient.astype(jnp.bfloat16)
    gradient_blocks = code_grad_low.reshape(groups, group_rows, ADAPTER_RANK)

    def backward_input(block):
        gradient_rows, table_row_list = block
        return jnp.einsum("hl,hle->he", gradient_rows.astype(jnp.float32), adapter_input_factor[table_row_list].astype(jnp.float32))

    adapter_input_rows = lax.map(backward_input, (gradient_blocks, table_row_blocks)).reshape(tokens.shape[0], MODEL_WIDTH)
    input_gradient = (jnp.dot(gate_grad, gate_up_weight[:, 0, :].T, preferred_element_type=jnp.float32)
               + jnp.dot(up_grad, gate_up_weight[:, 1, :].T, preferred_element_type=jnp.float32)
               + adapter_input_rows).astype(jnp.bfloat16)

    def add_grads(running_totals, block):
        input_total, output_total = running_totals
        token_row_block, codes_per_row, gradient_rows, up_weight_rows, table_row_list = block
        input_total = input_total.at[table_row_list].add(jnp.einsum("rk,rd->rkd", gradient_rows.astype(jnp.float32), token_row_block.astype(jnp.float32)))
        output_total = output_total.at[table_row_list].add(jnp.einsum("rk,rf->rkf", codes_per_row.astype(jnp.float32), up_weight_rows.astype(jnp.float32)))
        return (input_total, output_total), None

    start_totals = (jnp.zeros((ADAPTER_COUNT, ADAPTER_RANK, MODEL_WIDTH), jnp.float32), jnp.zeros((ADAPTER_COUNT, ADAPTER_RANK, HIDDEN_UNITS), jnp.float32))
    running_totals, unused = lax.scan(add_grads, start_totals, (token_blocks, code_blocks, gradient_blocks, up_weight_blocks, table_row_blocks))
    adapter_input_gradient = running_totals[0].astype(jnp.bfloat16)
    adapter_output_gradient = (adapter_scale * running_totals[1]).astype(jnp.bfloat16)
    return (layer_output, input_gradient, adapter_input_gradient, adapter_output_gradient)
```

```python
import jax
import jax.numpy as jnp
from jax import lax
from jax.sharding import PartitionSpec as P

adapter_scale = 0.5
chunk_count = 4
lane = 128
f32 = jnp.float32
bf16 = jnp.bfloat16


def pair_swap(x, axis):
    n = lax.axis_size(axis)
    return lax.ppermute(x, axis, [(i, i ^ 1) for i in range(n)])


def major_shift(x, axis, step):
    n = lax.axis_size(axis)
    m = n // 2
    return lax.ppermute(x, axis, [(i, (i // 2 + step) % m * 2 + i % 2) for i in range(n)])


def flip_minor(x, axis, dim):
    return jnp.where(lax.axis_index(axis) % 2 == 0, x, jnp.flip(x, dim))


def to_local(x, axis):
    n = lax.axis_size(axis)
    m = n // 2
    x = x.reshape((m, 2) + x.shape[1:])
    x = lax.dynamic_slice_in_dim(jnp.concatenate([x, x], 0), lax.axis_index(axis) // 2, m, 0)
    x = jnp.moveaxis(flip_minor(x, axis, 1), 1, 0)
    return x.reshape((n,) + x.shape[2:])


def to_global(x, axis):
    n = lax.axis_size(axis)
    m = n // 2
    x = jnp.moveaxis(x.reshape((2, m) + x.shape[1:]), 0, 1)
    x = flip_minor(x, axis, 1)
    start = (m - lax.axis_index(axis) // 2) % m
    x = lax.dynamic_slice_in_dim(jnp.concatenate([x, x], 0), start, m, 0)
    return x.reshape((n,) + x.shape[2:])


def local_sum(x, axis, wire):
    n = lax.axis_size(axis)
    m = n // 2
    half = x.shape[0] // 2
    block = half // m
    summed = x[:half] + pair_swap(x[half:].astype(wire), axis).astype(f32)
    total = summed[:block]
    for s in range(1, m):
        piece = summed[s * block:(s + 1) * block].astype(wire)
        total = total + major_shift(piece, axis, s).astype(f32)
    return total


def local_gather(x, axis):
    n = lax.axis_size(axis)
    m = n // 2
    blocks = [x] + [major_shift(x, axis, -s) for s in range(1, m)]
    half = jnp.concatenate(blocks, axis=1)
    return half, pair_swap(half, axis)


def sum_everywhere(x):
    for axis in ("tensor", "dp"):
        n = lax.axis_size(axis)
        if n & (n - 1):
            x = lax.psum(x, axis)
            continue
        bit = 1
        while bit < n:
            x = x + lax.ppermute(x, axis, [(i, i ^ bit) for i in range(n)])
            bit *= 2
    return x


def row_slots(request_token_rows, request_adapter, adapter_table_row, group_rows):
    request_count = request_token_rows.shape[1]
    run_ends = jnp.cumsum(request_token_rows, axis=1)
    position = jnp.arange(group_rows, dtype=jnp.int32)
    request_of = jnp.sum(
        (run_ends[:, None, :] <= position[None, :, None]).astype(jnp.int32), axis=2
    )
    adapter_ids = jnp.arange(adapter_table_row.shape[0], dtype=jnp.int32)
    table_row = jnp.sum(
        jnp.where(
            request_adapter[:, :, None] == adapter_ids[None, None, :],
            adapter_table_row[None, None, :],
            0,
        ),
        axis=2,
    )
    request_ids = jnp.arange(request_count, dtype=jnp.int32)
    return jnp.sum(
        jnp.where(request_of[:, :, None] == request_ids, table_row[:, None, :], 0), axis=2
    )


def slot_mask(slots, first_row, table_rows, rank):
    column = lax.broadcasted_iota(jnp.int32, (slots.shape[0], table_rows * rank), 1)
    return column // rank == (slots - first_row)[:, None]


def rank_spread(table_rows, rank, dtype):
    column = lax.broadcasted_iota(jnp.int32, (rank, table_rows * rank), 1)
    row = lax.broadcasted_iota(jnp.int32, (rank, table_rows * rank), 0)
    return (column % rank == row).astype(dtype)


def spread_codes(codes, mask, rank):
    spread = rank_spread(mask.shape[1] // rank, rank, bf16)
    tiled = jnp.dot(codes, spread, preferred_element_type=f32)
    return jnp.where(mask, tiled, 0.0).astype(bf16)


def fold_codes(full, mask, rank):
    spread = rank_spread(mask.shape[1] // rank, rank, f32)
    kept = jnp.where(mask, full, 0.0)
    return lax.dot_general(
        kept, spread, (((1,), (1,)), ((), ())), precision=lax.Precision.HIGHEST
    )


def chunk_bounds(width):
    tiles = max(width // lane, 1)
    count = min(chunk_count, tiles)
    ends = [tiles * i // count * lane for i in range(count)] + [width]
    return list(zip(ends[:-1], ends[1:]))


def on_device(
    tokens,
    output_gradient,
    gate_up_weight,
    down_weight,
    adapter_input_factor,
    adapter_output_factor,
    request_token_rows,
    request_adapter,
    adapter_table_row,
):
    group_rows = tokens.shape[0]
    groups = lax.axis_size("dp")
    rows = groups * group_rows
    rank = adapter_input_factor.shape[1]
    hidden_portion, width = down_weight.shape
    in_rows = adapter_input_factor.shape[0]
    out_rows = adapter_output_factor.shape[0]
    in_table = adapter_input_factor.reshape(in_rows * rank, width)
    out_table = adapter_output_factor.reshape(out_rows * rank, hidden_portion)
    bounds = chunk_bounds(hidden_portion)

    def spread_rows(x):
        x = lax.all_to_all(x, "dp", split_axis=1, concat_axis=0, tiled=True)
        return to_local(x.reshape(groups, group_rows, width), "dp").reshape(rows, width)

    grad_cols = spread_rows(output_gradient)
    token_cols = spread_rows(tokens)

    hidden_grads = []
    for low, high in bounds:
        part = lax.dot_general(
            grad_cols, down_weight[low:high], (((1,), (1,)), ((), ())),
            preferred_element_type=f32,
        )
        hidden_grads.append(local_sum(part, "dp", bf16))

    slots = row_slots(request_token_rows, request_adapter, adapter_table_row, group_rows)
    slots = to_local(slots, "dp").reshape(rows)
    in_mask = slot_mask(slots, lax.axis_index("tensor") * in_rows, in_rows, rank)
    out_mask = slot_mask(slots, lax.axis_index("dp") * out_rows, out_rows, rank)

    def total_codes(partial):
        partial = to_global(partial.reshape(groups, group_rows * rank), "dp")
        return to_local(sum_everywhere(partial), "dp").reshape(rows, rank)

    all_codes = lax.dot_general(
        token_cols, in_table, (((1,), (1,)), ((), ())), preferred_element_type=f32
    )
    code_low = total_codes(fold_codes(all_codes, in_mask, rank)).astype(bf16)
    code_wide = spread_codes(code_low, out_mask, rank)

    layer_part = jnp.zeros((rows, width), f32)
    input_part = jnp.zeros((rows, width), f32)
    code_part = jnp.zeros((rows, out_rows * rank), f32)
    up_grads = []
    for (low, high), hidden_grad in zip(bounds, hidden_grads):
        both = jnp.einsum(
            "rd,dgf->grf", token_cols, gate_up_weight[:, :, low:high],
            preferred_element_type=f32,
        )
        lifted = jnp.dot(code_wide, out_table[:, low:high], preferred_element_type=f32)
        gate_pre = local_sum(both[0], "dp", bf16)
        up_pre = local_sum(both[1] + adapter_scale * lifted, "dp", bf16)
        sig = jax.nn.sigmoid(gate_pre)
        hidden = (gate_pre * sig * up_pre).astype(bf16)
        gate_grad = (hidden_grad * up_pre * sig * (1.0 + gate_pre * (1.0 - sig))).astype(bf16)
        up_grad = (hidden_grad * gate_pre * sig).astype(bf16)
        near, far = local_gather(jnp.stack([hidden, up_grad, gate_grad]), "dp")
        full = jnp.concatenate([near, far], axis=1)
        layer_part = layer_part + jnp.dot(
            full[0], down_weight[low:high], preferred_element_type=f32
        )
        up_grads.append(full[1])
        code_part = code_part + lax.dot_general(
            full[1], out_table[:, low:high], (((1,), (1,)), ((), ())),
            preferred_element_type=f32,
        )
        grads = jnp.stack([full[2], full[1]])
        input_part = input_part + jnp.einsum(
            "grf,dgf->rd", grads, gate_up_weight[:, :, low:high],
            preferred_element_type=f32,
        )

    def finish(part):
        part = to_global(part.reshape(groups, group_rows, width), "dp")
        owners = lax.axis_size("tensor")
        part = to_local(part.reshape(owners, rows // owners, width), "tensor")
        return local_sum(part.reshape(rows, width), "tensor", f32).astype(bf16)

    layer_output = finish(layer_part)
    code_grad = adapter_scale * total_codes(fold_codes(code_part, out_mask, rank))
    grad_wide = spread_codes(code_grad.astype(bf16), in_mask, rank)
    input_part = input_part + jnp.dot(grad_wide, in_table, preferred_element_type=f32)
    input_gradient = finish(input_part)
    adapter_input_gradient = lax.dot_general(
        grad_wide, token_cols, (((0,), (0,)), ((), ())), preferred_element_type=f32
    ).astype(bf16).reshape(in_rows, rank, width)
    up_grad = jnp.concatenate(up_grads, axis=1)
    adapter_output_gradient = (
        adapter_scale
        * lax.dot_general(
            code_wide, up_grad, (((0,), (0,)), ((), ())), preferred_element_type=f32
        )
    ).astype(bf16).reshape(out_rows, rank, hidden_portion)
    return (layer_output, input_gradient, adapter_input_gradient, adapter_output_gradient)


def solution(mesh):
    in_specs = (
        P("dp", None),
        P("dp", None),
        P("dp", None, "tensor"),
        P("tensor", "dp"),
        P("tensor", None, "dp"),
        P("dp", None, "tensor"),
        P(),
        P(),
        P(),
    )
    out_specs = (
        P("tensor", "dp"),
        P("tensor", "dp"),
        P("tensor", None, "dp"),
        P("dp", None, "tensor"),
    )
    return jax.shard_map(
        on_device, mesh=mesh, in_specs=in_specs, out_specs=out_specs, check_vma=False
    )
```
